32 devices in a mesh: fsdp: 32 (over z, y, x, core).
Axes of the slice: x: 2, y: 2, z: 4, core: 2. Of those that a mesh axis runs over, the one named last changes fastest.
Arguments:
- images: bfloat16 [64, 197, 384], P('fsdp'), may hold values from -6 to 6
- cotangent: float32 [64, 197, 384], P('fsdp'), may hold values from -6 to 6
- counts: int32 [32], P('fsdp'), may hold values from 1 to 2, as said below
- params: float32 [2, 1777664], P(None, 'fsdp'), may hold values from -3 to 3, as said below
- moment_one: float32 [2, 1777664], P(None, 'fsdp'), may hold values from -12 to 12
- moment_two: float32 [2, 1777664], P(None, 'fsdp'), may hold values from 20 to 400
Outputs:
- outputs: float32 [64, 197, 384], P('fsdp')
- input_grad: float32 [64, 197, 384], P('fsdp')
- weight_grads: float32 [2, 1777664], P(None, 'fsdp')
- new_params: float32 [2, 1777664], P(None, 'fsdp')
- new_first: float32 [2, 1777664], P(None, 'fsdp')
- new_second: float32 [2, 1777664], P(None, 'fsdp')
The draws below stay inside these ranges and needn't reach their ends.
Inputs may be any that keep to these rules, and one draw needn't show every extreme that they name: Each device's images fill its first counts slots, the others are empty; some device holds 2 images and some holds 1. `params`: each row is one layer's parameters in the order of the steps; entries past 1774080 are zero.
All inputs are finite; a program needn't handle non-finite values.
Results may differ from the reference program's by a relative error of at most 0.012.
The reference program's roundings to bfloat16 on the way count: a program that leaves them out, or rounds other values in their place, can miss the bound.
Values may be sent and summed in bfloat16 or wider, within the bound.
A program may use at most 128 MiB of HBM per device.

```python
import math
import jax
import jax.numpy as jnp
from jax import lax

D = 384
HEADS = 6
HEAD_DIM = 64
FF = 1536
SEQ = 197
LAYERS = 2
ADAM_STEP = 4
IMG_DEV = 2
SLOTS = 64
PARAMS = 1774080
PFLAT = 1777664
N_FSDP = 32


def draw_counts(key, part):
    key_load, key_busy, key_light = jax.random.split(key, 3)
    device_loads = jax.random.randint(key_load, (N_FSDP,), 1, IMG_DEV + 1)
    busiest = jax.random.randint(key_busy, (), 0, N_FSDP)
    lightest = (busiest + jax.random.randint(key_light, (), 1, N_FSDP)) % N_FSDP
    return device_loads.at[busiest].set(IMG_DEV).at[lightest].set(1).astype(jnp.int32)


def draw_params(key, part):
    position = jnp.arange(PFLAT)
    noise = jnp.clip(jax.random.normal(key, (LAYERS, PFLAT), jnp.float32), -6.0, 6.0)
    square = D * D
    start_out = 3 * square
    start_one = 4 * square
    start_two = 4 * square + D * FF
    start_small = 4 * square + 2 * D * FF
    scale_vec = jnp.where(position < start_out, D ** (-0.5), jnp.where(position < start_one, 6.0 * D ** (-0.5), jnp.where(position < start_two, D ** (-0.5), jnp.where(position < start_small, FF ** (-0.5), 0.5))))
    gain_one = (position >= start_small) & (position < start_small + D)
    gain_two = (position >= start_small + 5 * D) & (position < start_small + 6 * D)
    is_gain = gain_one | gain_two
    scale_vec = jnp.where(is_gain, 0.1, scale_vec)
    scale_vec = jnp.where(position >= PARAMS, 0.0, scale_vec)
    gain_add = jnp.where(position >= PARAMS, 0.0, is_gain.astype(jnp.float32))
    return noise * scale_vec[None, :] + gain_add[None, :]


def block_levels(rng, extent, shards, low, top_value):
    def one(dim, shards_of):
        draws = jax.random.uniform(jax.random.fold_in(jax.random.fold_in(rng, 6), dim), (shards_of,), jnp.float32, low / len(shards), top_value / len(shards))
        return jnp.repeat(jnp.exp(draws), extent[dim] // shards_of).reshape((-1,) + (1,) * (len(extent) - dim - 1))

    factor_of = one(*shards[0])
    for cut in shards[1:]:
        factor_of = factor_of * one(*cut)
    return factor_of


def scatter_about(key, extent, deviation, limit, cuts=(), kind=jnp.bfloat16):
    loudness = block_levels(key, extent, cuts, -0.22, 0.18) if cuts else 1.0
    values = jax.random.normal(key, extent, jnp.float32) * deviation * loudness
    return jnp.minimum(jnp.maximum(values, -limit), limit).astype(kind)


def setup_inputs(seed: int = 0) -> dict:
    seeds = jax.random.split(jax.random.key(seed), 7)
    images = scatter_about(seeds[0], (SLOTS, SEQ, D), 1.0, 6.0, ((0, 32),))
    cotangent = scatter_about(seeds[1], (SLOTS, SEQ, D), 1.0, 6.0, ((0, 32),), jnp.float32)
    counts = draw_counts(jax.random.fold_in(seeds[6], 71), 0)
    params = draw_params(jax.random.fold_in(seeds[6], 71), 0)
    moment_one = scatter_about(seeds[4], (LAYERS, PFLAT), 2.0, 12.0, ((1, 32),), jnp.float32)
    moment_two = jnp.clip(jnp.exp(math.log(400.0) - 2.9957323 * jax.random.uniform(seeds[5], (LAYERS, PFLAT), jnp.float32) ** block_levels(seeds[5], (LAYERS, PFLAT), ((1, 32),), -0.2, 0.2)), 20.0, 400.0)
    return dict(images=images, cotangent=cotangent, counts=counts, params=params, moment_one=moment_one, moment_two=moment_two)


EPS_NORM = 1e-06
BETA_ONE = 0.9
BETA_TWO = 0.999
ADAM_EPS = 1e-08
DECAY = 0.05
LEARN = 0.2
INV_ROOT_TWO = 0.7071067811865476
INV_ROOT_TAU = 0.3989422804014327

def layout():
    return [('w_qkv', (D, 3 * D)), ('w_out', (D, D)), ('w_one', (D, FF)), ('w_two', (FF, D)), ('gain_one', (D,)), ('bias_one', (D,)), ('bias_query', (D,)), ('bias_value', (D,)), ('bias_out', (D,)), ('gain_two', (D,)), ('bias_two', (D,)), ('bias_hidden', (FF,)), ('bias_mlp', (D,))]

def unpack(flat_vec):
    pieces = {}
    offset = 0
    for param_name, param_shape in layout():
        entries = math.prod(param_shape)
        pieces[param_name] = flat_vec[offset:offset + entries].reshape(param_shape)
        offset = offset + entries
    return pieces

def pack(pieces, length_total):
    flat_vec = jnp.concatenate([pieces[param_name].reshape(-1) for param_name, param_shape in layout()])
    return jnp.pad(flat_vec, (0, length_total - flat_vec.shape[0]))

def project(left, right):
    return jnp.dot(left, right, preferred_element_type=jnp.float32)

def batched(form, left, right):
    return jnp.einsum(form, left.astype(jnp.float32), right.astype(jnp.float32))

def normalize(rows_in, gain_vec, shift_vec):
    centre = rows_in - lax.optimization_barrier(jnp.mean(rows_in, axis=-1, keepdims=True))
    spread = lax.rsqrt(lax.optimization_barrier(jnp.mean(centre * centre, axis=-1, keepdims=True)) + EPS_NORM)
    normed = centre * spread
    return (normed, spread, normed * gain_vec.astype(jnp.float32) + shift_vec.astype(jnp.float32))

def normalize_back(upstream, normed, spread, gain_vec):
    scaled = upstream * gain_vec.astype(jnp.float32)
    centred = scaled - lax.optimization_barrier(jnp.mean(scaled, axis=-1, keepdims=True)) - normed * lax.optimization_barrier(jnp.mean(scaled * normed, axis=-1, keepdims=True))
    return (spread * centred, lax.optimization_barrier(jnp.sum(upstream * normed, axis=0)), lax.optimization_barrier(jnp.sum(upstream, axis=0)))

def gelu_slope(pre_act):
    return 0.5 * (1.0 + lax.erf(pre_act * INV_ROOT_TWO)) + pre_act * INV_ROOT_TAU * jnp.exp(-0.5 * pre_act * pre_act)

def split_heads(rows_in):
    return rows_in.reshape(rows_in.shape[0] // SEQ, SEQ, HEADS, HEAD_DIM)

def attention_scores(query_rows, key_rows):
    return batched('bqhc,bkhc->bhqk', split_heads(query_rows), split_heads(key_rows)) * HEAD_DIM ** (-0.5)

def layer_forward(stream, weights):
    normed_one, spread_one, pre_one = normalize(stream, weights['gain_one'], weights['bias_one'])
    act_one = pre_one.astype(jnp.bfloat16)
    qkv_rows = project(act_one, weights['w_qkv'])
    query_rows = (qkv_rows[:, :D] + weights['bias_query'].astype(jnp.float32)).astype(jnp.bfloat16)
    key_rows = qkv_rows[:, D:2 * D].astype(jnp.bfloat16)
    value_rows = (qkv_rows[:, 2 * D:] + weights['bias_value'].astype(jnp.float32)).astype(jnp.bfloat16)
    scores = attention_scores(query_rows, key_rows)
    row_max = lax.optimization_barrier(jnp.max(scores, axis=-1, keepdims=True))
    log_total = row_max + jnp.log(lax.optimization_barrier(jnp.sum(jnp.exp(scores - row_max), axis=-1, keepdims=True)))
    attn_probs = jnp.exp(scores - log_total).astype(jnp.bfloat16)
    attended = batched('bhqk,bkhc->bqhc', attn_probs, split_heads(value_rows)).reshape(-1, D).astype(jnp.bfloat16)
    middle = stream + project(attended, weights['w_out']) + weights['bias_out'].astype(jnp.float32)
    normed_two, spread_two, pre_two = normalize(middle, weights['gain_two'], weights['bias_two'])
    act_two = pre_two.astype(jnp.bfloat16)
    hidden_pre = project(act_two, weights['w_one']) + weights['bias_hidden'].astype(jnp.float32)
    hidden_act = jax.nn.gelu(hidden_pre, approximate=False).astype(jnp.bfloat16)
    result = middle + project(hidden_act, weights['w_two']) + weights['bias_mlp'].astype(jnp.float32)
    saved = (normed_one, spread_one, act_one, query_rows, key_rows, value_rows, log_total, attended, normed_two, spread_two, act_two, hidden_pre, hidden_act)
    return (result, saved)

def layer_backward(upstream, saved, weights):
    normed_one, spread_one, act_one, query_rows, key_rows, value_rows, log_total, attended, normed_two, spread_two, act_two, hidden_pre, hidden_act = saved
    grad_parts = {}
    up_bf = upstream.astype(jnp.bfloat16)
    grad_parts['w_two'] = project(hidden_act.T, up_bf)
    grad_parts['bias_mlp'] = lax.optimization_barrier(jnp.sum(upstream, axis=0))
    hidden_grad = project(up_bf, weights['w_two'].T) * gelu_slope(hidden_pre)
    hidden_bf = hidden_grad.astype(jnp.bfloat16)
    grad_parts['w_one'] = project(act_two.T, hidden_bf)
    grad_parts['bias_hidden'] = lax.optimization_barrier(jnp.sum(hidden_grad, axis=0))
    norm_grad, grad_parts['gain_two'], grad_parts['bias_two'] = normalize_back(project(hidden_bf, weights['w_one'].T), normed_two, spread_two, weights['gain_two'])
    middle_grad = upstream + norm_grad
    middle_bf = middle_grad.astype(jnp.bfloat16)
    grad_parts['w_out'] = project(attended.T, middle_bf)
    grad_parts['bias_out'] = lax.optimization_barrier(jnp.sum(middle_grad, axis=0))
    attended_grad = project(middle_bf, weights['w_out'].T).astype(jnp.bfloat16)
    heads_do = split_heads(attended_grad)
    attn_exact = jnp.exp(attention_scores(query_rows, key_rows) - log_total)
    attn_probs = attn_exact.astype(jnp.bfloat16)
    value_grad = batched('bhqk,bqhc->bkhc', attn_probs, heads_do).reshape(-1, D)
    prob_grad = batched('bqhc,bkhc->bhqk', heads_do, split_heads(value_rows))
    row_inner = lax.optimization_barrier(jnp.sum(prob_grad * attn_exact, axis=-1, keepdims=True))
    score_grad = (attn_exact * (prob_grad - row_inner) * HEAD_DIM ** (-0.5)).astype(jnp.bfloat16)
    query_grad = batched('bhqk,bkhc->bqhc', score_grad, split_heads(key_rows)).reshape(-1, D)
    key_grad = batched('bhqk,bqhc->bkhc', score_grad, split_heads(query_rows)).reshape(-1, D)
    grad_parts['bias_query'] = lax.optimization_barrier(jnp.sum(query_grad, axis=0))
    grad_parts['bias_value'] = lax.optimization_barrier(jnp.sum(value_grad, axis=0))
    mixed_bf = jnp.concatenate([query_grad, key_grad, value_grad], axis=1).astype(jnp.bfloat16)
    grad_parts['w_qkv'] = project(act_one.T, mixed_bf)
    in_grad, grad_parts['gain_one'], grad_parts['bias_one'] = normalize_back(project(mixed_bf, weights['w_qkv'].T), normed_one, spread_one, weights['gain_one'])
    return (middle_grad + in_grad, grad_parts)

def adamw(weights_in, first_in, second_in, grad_in):
    first_new = BETA_ONE * first_in + (1.0 - BETA_ONE) * grad_in
    second_new = BETA_TWO * second_in + (1.0 - BETA_TWO) * grad_in * grad_in
    first_hat = first_new / (1.0 - BETA_ONE ** ADAM_STEP)
    second_hat = second_new / (1.0 - BETA_TWO ** ADAM_STEP)
    updated = weights_in - LEARN * (first_hat / (jnp.sqrt(second_hat) + ADAM_EPS) + DECAY * weights_in)
    return (updated, first_new, second_new)

def reference(images, cotangent, counts, params, moment_one, moment_two):
    layer_weights = [unpack(params[position].astype(jnp.bfloat16)) for position in range(LAYERS)]
    live = (jnp.arange(IMG_DEV)[None, :] < counts[:, None]).astype(jnp.float32)
    grouped_in = images.reshape(N_FSDP, IMG_DEV * SEQ, D)
    grouped_cot = cotangent.reshape(N_FSDP, IMG_DEV * SEQ, D)

    def step_block(totals, inputs):
        block_in, block_cot, block_live = inputs
        live_rows = jnp.repeat(block_live, SEQ)[:, None]
        stream = block_in.astype(jnp.float32)
        saves = []
        for position in range(LAYERS):
            stream, saved = layer_forward(stream, layer_weights[position])
            saves.append(saved)
        output_rows = stream * live_rows
        upstream = block_cot * live_rows
        flats = [None] * LAYERS
        for position in reversed(range(LAYERS)):
            upstream, grad_parts = layer_backward(upstream, saves[position], layer_weights[position])
            flats[position] = pack(grad_parts, PFLAT)
        return (totals + jnp.stack(flats), (output_rows, upstream))
    totals, (output_rows, grad_rows) = lax.scan(step_block, jnp.zeros((LAYERS, PFLAT), jnp.float32), (grouped_in, grouped_cot, live))
    updated, first_new, second_new = adamw(params, moment_one, moment_two, totals)
    return (output_rows.reshape(SLOTS, SEQ, D), grad_rows.reshape(SLOTS, SEQ, D), totals, updated, first_new, second_new)
```

```python
import functools
import math

import jax
import jax.numpy as jnp
from jax import lax
from jax.experimental import pallas as pl
from jax.experimental.pallas import tpu as pltpu
from jax.sharding import PartitionSpec as P

D = 384
HEADS = 6
HEAD_DIM = 64
FF = 1536
SEQ = 197
LAYERS = 2
ADAM_STEP = 4

EPS_NORM = 1e-06
BETA_ONE = 0.9
BETA_TWO = 0.999
ADAM_EPS = 1e-08
DECAY = 0.05
LEARN = 0.2
INV_ROOT_TWO = 0.7071067811865476
INV_ROOT_TAU = 0.3989422804014327
LANES = 128
ROWS = 208
SUB = D // LANES
CHUNKS = FF // D
F32 = jnp.float32
BF16 = jnp.bfloat16

AT_OUT = 3 * D * SUB
AT_ONE = AT_OUT + D * SUB
AT_TWO = AT_ONE + D * SUB * CHUNKS
AT_SMALL = AT_TWO + D * SUB * CHUNKS
BLOCKS = 4 + 2 * CHUNKS
G_ONE, B_ONE, B_QUERY, B_VALUE, B_OUT, G_TWO, B_TWO, B_HIDDEN = range(8)
B_MLP = B_HIDDEN + CHUNKS
VECTORS = B_MLP + 1
USED = AT_SMALL + VECTORS * SUB


def nn(left, right):
    return jnp.dot(left, right, preferred_element_type=F32)


def nt(left, right):
    return lax.dot_general(left, right, (((1,), (1,)), ((), ())), preferred_element_type=F32)


def tn(left, right):
    return lax.dot_general(left, right, (((0,), (0,)), ((), ())), preferred_element_type=F32)


def block_rows(block, tile):
    if block < 3:
        return block * SUB + tile, 3 * SUB
    if block == 3:
        return AT_OUT + tile, SUB
    if block < 4 + CHUNKS:
        return AT_ONE + (block - 4) * SUB + tile, CHUNKS * SUB
    return AT_TWO + (block - 4 - CHUNKS) * D * SUB + tile, SUB


def unpack(gathered, flat, mats, vecs):
    devices, rows = gathered.shape[0], gathered.shape[1]

    def widen(device, carry):
        flat[pl.ds(device * rows, rows), :] = gathered[device].astype(F32)
        return carry

    lax.fori_loop(0, devices, widen, 0)
    for block in range(BLOCKS):
        for tile in range(SUB):
            start, stride = block_rows(block, tile)
            mats[block, :, tile * LANES : (tile + 1) * LANES] = flat[
                pl.ds(start, D, stride=stride), :
            ].astype(BF16)
    for vector in range(VECTORS):
        for tile in range(SUB):
            row = AT_SMALL + vector * SUB + tile
            vecs[vector : vector + 1, tile * LANES : (tile + 1) * LANES] = flat[row : row + 1, :]


def put_block(flat, block, value):
    for tile in range(SUB):
        start, stride = block_rows(block, tile)
        flat[pl.ds(start, D, stride=stride), :] = value[:, tile * LANES : (tile + 1) * LANES]


def put_vector(flat, vector, value):
    for tile in range(SUB):
        row = AT_SMALL + vector * SUB + tile
        flat[row : row + 1, :] = value[:, tile * LANES : (tile + 1) * LANES]


def col_sum(value):
    return jnp.sum(value, axis=0, keepdims=True)


def normalize(rows_in):
    centre = rows_in - jnp.mean(rows_in, axis=-1, keepdims=True)
    spread = lax.rsqrt(jnp.mean(centre * centre, axis=-1, keepdims=True) + EPS_NORM)
    return centre * spread, spread


def normalize_back(upstream, normed, spread, gain_vec):
    scaled = upstream * gain_vec
    centred = (
        scaled
        - jnp.mean(scaled, axis=-1, keepdims=True)
        - normed * jnp.mean(scaled * normed, axis=-1, keepdims=True)
    )
    return spread * centred


def lane_pick(half):
    lane = lax.broadcasted_iota(jnp.int32, (ROWS, LANES), 1)
    return (lane < HEAD_DIM) if half == 0 else (lane >= HEAD_DIM)


def pick(value, half):
    return jnp.where(lane_pick(half), value, jnp.zeros_like(value))


def forward(slots, stream, mats, vecs, saves):
    query, key, value, attended, exact, middle, slope, hidden = saves

    def vec(index):
        return vecs[index : index + 1, :]

    normed, _ = normalize(stream[...].astype(F32))
    act = (normed * vec(G_ONE) + vec(B_ONE)).astype(BF16)
    query[...] = (nn(act, mats[0]) + vec(B_QUERY)).astype(BF16)
    key[...] = nn(act, mats[1]).astype(BF16)
    value[...] = (nn(act, mats[2]) + vec(B_VALUE)).astype(BF16)

    def heads(pair, carry):
        lanes = pl.ds(pl.multiple_of(pair * LANES, LANES), LANES)
        inside = lax.broadcasted_iota(jnp.int32, (ROWS, ROWS), 1) < SEQ
        for slot in range(slots):
            rows = pl.ds(slot * ROWS, ROWS)
            q_pair, k_pair, v_pair = query[rows, lanes], key[rows, lanes], value[rows, lanes]
            total = jnp.zeros((ROWS, LANES), F32)
            for half in range(2):
                scores = nt(pick(q_pair, half), k_pair) * HEAD_DIM ** (-0.5)
                scores = jnp.where(inside, scores, -1e30)
                expd = jnp.exp(scores - jnp.max(scores, axis=-1, keepdims=True))
                probs = expd * (1.0 / jnp.sum(expd, axis=-1, keepdims=True))
                exact[pair * (2 * slots) + 2 * slot + half] = probs
                total += pick(nn(probs.astype(BF16), v_pair), half)
            attended[rows, lanes] = total.astype(BF16)
        return carry

    lax.fori_loop(0, HEADS // 2, heads, 0)
    middle[...] = stream[...].astype(F32) + nn(attended[...], mats[3]) + vec(B_OUT)
    normed, _ = normalize(middle[...])
    act = (normed * vec(G_TWO) + vec(B_TWO)).astype(BF16)

    result = middle[...] + vec(B_MLP)
    for chunk in range(CHUNKS):
        pre = nn(act, mats[4 + chunk]) + vec(B_HIDDEN + chunk)
        below = 0.5 * (1.0 + lax.erf(pre * INV_ROOT_TWO))
        hidden[chunk] = (pre * below).astype(BF16)
        slope[chunk] = below + pre * INV_ROOT_TAU * jnp.exp(-0.5 * pre * pre)
        result += nn(hidden[chunk], mats[4 + CHUNKS + chunk])
    return result


def backward(slots, upstream, stream, mats, vecs, saves, flat, mixed, att_grad):
    query, key, value, attended, exact, middle, slope, hidden = saves

    def vec(index):
        return vecs[index : index + 1, :]

    grad = upstream[...]
    up_bf = grad.astype(BF16)
    put_vector(flat, B_MLP, col_sum(grad))
    normed, spread = normalize(middle[...])
    act = (normed * vec(G_TWO) + vec(B_TWO)).astype(BF16)
    into = jnp.zeros_like(grad)
    for chunk in range(CHUNKS):
        hidden_grad = nt(up_bf, mats[4 + CHUNKS + chunk]) * slope[chunk]
        hidden_bf = hidden_grad.astype(BF16)
        put_vector(flat, B_HIDDEN + chunk, col_sum(hidden_grad))
        put_block(flat, 4 + CHUNKS + chunk, tn(hidden[chunk], up_bf))
        put_block(flat, 4 + chunk, tn(act, hidden_bf))
        into += nt(hidden_bf, mats[4 + chunk])
    put_vector(flat, G_TWO, col_sum(into * normed))
    put_vector(flat, B_TWO, col_sum(into))
    middle[...] = grad + normalize_back(into, normed, spread, vec(G_TWO))
    middle_bf = middle[...].astype(BF16)
    put_vector(flat, B_OUT, col_sum(middle[...]))
    put_block(flat, 3, tn(attended[...], middle_bf))
    att_grad[...] = nt(middle_bf, mats[3]).astype(BF16)

    def heads(pair, carry):
        lanes = pl.ds(pl.multiple_of(pair * LANES, LANES), LANES)
        q_sum = jnp.zeros((1, LANES), F32)
        v_sum = jnp.zeros((1, LANES), F32)
        for slot in range(slots):
            rows = pl.ds(slot * ROWS, ROWS)
            q_pair, k_pair, v_pair = query[rows, lanes], key[rows, lanes], value[rows, lanes]
            out_pair = att_grad[rows, lanes]
            q_grad = jnp.zeros((ROWS, LANES), F32)
            k_grad = jnp.zeros((ROWS, LANES), F32)
            v_grad = jnp.zeros((ROWS, LANES), F32)
            for half in range(2):
                probs = exact[pair * (2 * slots) + 2 * slot + half]
                out_half = pick(out_pair, half)
                v_grad += tn(probs.astype(BF16), out_half)
                prob_grad = nt(out_half, v_pair)
                inner = jnp.sum(prob_grad * probs, axis=-1, keepdims=True)
                score_grad = (probs * (prob_grad - inner) * HEAD_DIM ** (-0.5)).astype(BF16)
                q_grad += nn(score_grad, pick(k_pair, half))
                k_grad += tn(score_grad, pick(q_pair, half))
            q_sum += col_sum(q_grad)
            v_sum += col_sum(v_grad)
            mixed[0, rows, lanes] = q_grad.astype(BF16)
            mixed[1, rows, lanes] = k_grad.astype(BF16)
            mixed[2, rows, lanes] = v_grad.astype(BF16)
        flat[pl.ds(AT_SMALL + B_QUERY * SUB + pair, 1), :] = q_sum
        flat[pl.ds(AT_SMALL + B_VALUE * SUB + pair, 1), :] = v_sum
        return carry

    lax.fori_loop(0, HEADS // 2, heads, 0)
    normed, spread = normalize(stream[...].astype(F32))
    act = (normed * vec(G_ONE) + vec(B_ONE)).astype(BF16)
    into = jnp.zeros_like(grad)
    for part in range(3):
        put_block(flat, part, tn(act, mixed[part]))
        into += nt(mixed[part], mats[part])
    put_vector(flat, G_ONE, col_sum(into * normed))
    put_vector(flat, B_ONE, col_sum(into))
    return middle[...] + normalize_back(into, normed, spread, vec(G_ONE))


def send_out(flat, packed):
    devices, rows = packed.shape[0], packed.shape[1]
    owned = flat.shape[0] // devices
    flat[USED:, :] = jnp.zeros((flat.shape[0] - USED, LANES), F32)

    def narrow(device, carry):
        packed[device, :owned, :] = flat[pl.ds(device * owned, owned), :].astype(BF16)
        if rows > owned:
            packed[device, owned:, :] = jnp.zeros((rows - owned, LANES), BF16)
        return carry

    lax.fori_loop(0, devices, narrow, 0)


def save_shapes(slots):
    tokens = slots * ROWS
    return [
        ((tokens, D), BF16),
        ((tokens, D), BF16),
        ((tokens, D), BF16),
        ((tokens, D), BF16),
        ((HEADS * slots, ROWS, ROWS), F32),
        ((tokens, D), F32),
        ((CHUNKS, tokens, D), F32),
        ((CHUNKS, tokens, D), BF16),
    ]


WEIGHTS = [((BLOCKS, D, D), BF16), ((16, D), F32)]


def first_kernel(slots, gathered, stream, *rest):
    mats, vecs, *saves = rest[:10]
    result, flat = rest[10:]
    unpack(gathered, flat, mats, vecs)
    result[...] = forward(slots, stream, mats, vecs, saves)


def turn_kernel(slots, gathered, stream, upstream, result, down, packed, *rest):
    flat, mixed, att_grad, mats, vecs, *saves = rest
    unpack(gathered, flat, mats, vecs)
    result[...] = forward(slots, stream, mats, vecs, saves)
    down[...] = backward(
        slots, upstream, stream, mats, vecs, saves, flat, mixed, att_grad
    )
    send_out(flat, packed)


def last_kernel(slots, upstream, stream, *rest):
    mats, vecs, *saved = rest[:10]
    down, packed, flat, mixed, att_grad, middle = rest[10:]
    middle[...] = saved[5][...]
    saved[5] = middle
    down[...] = backward(
        slots, upstream, stream, mats, vecs, saved, flat, mixed, att_grad
    )
    send_out(flat, packed)


def shapes(listed):
    return [jax.ShapeDtypeStruct(extent, kind) for extent, kind in listed]


def scratch(listed):
    return [pltpu.VMEM(extent, kind) for extent, kind in listed]


def call(body, args, outs, scratches, flops):
    whole = pl.BlockSpec(memory_space=pltpu.VMEM)
    return pl.pallas_call(
        body,
        out_shape=shapes(outs),
        in_specs=[whole] * len(args),
        out_specs=[whole] * len(outs),
        scratch_shapes=scratch(scratches),
        cost_estimate=pl.CostEstimate(flops=flops, bytes_accessed=12000000, transcendentals=0),
        compiler_params=pltpu.CompilerParams(vmem_limit_bytes=60000000),
    )(*args)


def adamw(weights_in, first_in, second_in, grad_in):
    first_new = BETA_ONE * first_in + (1.0 - BETA_ONE) * grad_in
    second_new = BETA_TWO * second_in + (1.0 - BETA_TWO) * grad_in * grad_in
    first_hat = first_new / (1.0 - BETA_ONE**ADAM_STEP)
    second_hat = second_new / (1.0 - BETA_TWO**ADAM_STEP)
    updated = weights_in - LEARN * (
        first_hat / (jnp.sqrt(second_hat) + ADAM_EPS) + DECAY * weights_in
    )
    return (updated, first_new, second_new)


def as_tiles(shard_vec):
    return shard_vec.astype(jnp.bfloat16).reshape(-1, LANES)


def on_device(images, cotangent, counts, params, moment_one, moment_two):
    slots = images.shape[0]
    shard_len = params.shape[1]
    devices = lax.axis_size("fsdp")
    owned = shard_len // LANES
    padded = -(-owned // 16) * 16
    tokens = slots * ROWS
    flat_rows = owned * devices
    live = (jnp.arange(slots) < counts[0]).astype(F32)[:, None, None]
    gathered = [
        lax.all_gather(as_tiles(params[position]), "fsdp", axis=0) for position in range(LAYERS)
    ]
    widen = ((0, 0), (0, ROWS - SEQ), (0, 0))
    start = jnp.pad(images, widen).reshape(tokens, D)
    upstream = jnp.pad(cotangent * live, widen).reshape(tokens, D)

    saves = save_shapes(slots)
    rows_out = ((tokens, D), F32)
    packed_out = ((devices, padded, LANES), BF16)
    flat = ((flat_rows, LANES), F32)
    back = [flat, ((3, tokens, D), BF16), ((tokens, D), BF16)]
    flops = 2 * tokens * USED * LANES

    *kept, stream = call(
        functools.partial(first_kernel, slots),
        [gathered[0], start],
        WEIGHTS + saves + [rows_out],
        [flat],
        flops,
    )
    result, down, packed_one = call(
        functools.partial(turn_kernel, slots),
        [gathered[1], stream, upstream],
        [rows_out, rows_out, packed_out],
        back + WEIGHTS + saves,
        3 * flops,
    )
    down, packed_zero = call(
        functools.partial(last_kernel, slots),
        [down, start] + kept,
        [rows_out, packed_out],
        back + [rows_out],
        2 * flops,
    )
    grad_stack = jnp.stack(
        [
            lax.psum_scatter(
                packed.reshape(devices * padded, LANES), "fsdp", scatter_dimension=0, tiled=True
            )[:owned]
            .astype(F32)
            .reshape(-1)
            for packed in (packed_zero, packed_one)
        ]
    )
    updated, first_new, second_new = adamw(params, moment_one, moment_two, grad_stack)
    return (
        result.reshape(slots, ROWS, D)[:, :SEQ] * live,
        down.reshape(slots, ROWS, D)[:, :SEQ],
        grad_stack,
        updated,
        first_new,
        second_new,
    )


def solution(mesh):
    placed = (
        P("fsdp", None, None),
        P("fsdp", None, None),
        P("fsdp"),
        P(None, "fsdp"),
        P(None, "fsdp"),
        P(None, "fsdp"),
    )
    return jax.shard_map(
        on_device,
        mesh=mesh,
        in_specs=placed,
        out_specs=(
            P("fsdp", None, None),
            P("fsdp", None, None),
            P(None, "fsdp"),
            P(None, "fsdp"),
            P(None, "fsdp"),
            P(None, "fsdp"),
        ),
        check_vma=False,
    )
```

```python
import functools
import math

import jax
import jax.numpy as jnp
from jax import lax
from jax.experimental import pallas as pl
from jax.experimental.pallas import tpu as pltpu
from jax.sharding import PartitionSpec as P

D = 384
HEADS = 6
HEAD_DIM = 64
FF = 1536
SEQ = 197
LAYERS = 2
ADAM_STEP = 4

EPS_NORM = 1e-06
BETA_ONE = 0.9
BETA_TWO = 0.999
ADAM_EPS = 1e-08
DECAY = 0.05
LEARN = 0.2
INV_ROOT_TWO = 0.7071067811865476
INV_ROOT_TAU = 0.3989422804014327
LANES = 128
ROWS = 208
SUB = D // LANES
CHUNKS = FF // D
F32 = jnp.float32
BF16 = jnp.bfloat16

AT_OUT = 3 * D * SUB
AT_ONE = AT_OUT + D * SUB
AT_TWO = AT_ONE + D * SUB * CHUNKS
AT_SMALL = AT_TWO + D * SUB * CHUNKS
BLOCKS = 4 + 2 * CHUNKS
G_ONE, B_ONE, B_QUERY, B_VALUE, B_OUT, G_TWO, B_TWO, B_HIDDEN = range(8)
B_MLP = B_HIDDEN + CHUNKS
VECTORS = B_MLP + 1
USED = AT_SMALL + VECTORS * SUB


def nn(left, right):
    return jnp.dot(left, right, preferred_element_type=F32)


def nt(left, right):
    return lax.dot_general(left, right, (((1,), (1,)), ((), ())), preferred_element_type=F32)


def tn(left, right):
    return lax.dot_general(left, right, (((0,), (0,)), ((), ())), preferred_element_type=F32)


def block_rows(block, tile):
    if block < 3:
        return block * SUB + tile, 3 * SUB
    if block == 3:
        return AT_OUT + tile, SUB
    if block < 4 + CHUNKS:
        return AT_ONE + (block - 4) * SUB + tile, CHUNKS * SUB
    return AT_TWO + (block - 4 - CHUNKS) * D * SUB + tile, SUB


def part_order(part, bits):
    order = list(range(bits))
    if part == 1 and bits > 2:
        order[1], order[2] = 2, 1
    return order


def owner_of(part, bits, position):
    owner = 0
    for place, bit in enumerate(part_order(part, bits)):
        owner = owner + (position // 2 ** (bits - 1 - place)) % 2 * 2**bit
    return owner


def position_of(part, bits, device):
    position = 0
    for place, bit in enumerate(part_order(part, bits)):
        position = position + device // 2**bit % 2 * 2 ** (bits - 1 - place)
    return position


def meet(bits, me):
    barrier = pltpu.get_barrier_semaphore()
    for bit in range(bits):
        pl.semaphore_signal(
            barrier, inc=1, device_id=(across(me, bit),), device_id_type=pl.DeviceIdType.MESH
        )
    pl.semaphore_wait(barrier, bits)


def across(me, bit):
    return me + 2**bit * (1 - 2 * (me // 2**bit % 2))


def gather_kernel(bits, *refs):
    pairs = LAYERS * 2
    own, out = refs[:pairs], refs[pairs : 2 * pairs]
    local_sem, send_sem, recv_sem = refs[2 * pairs :]
    me = lax.axis_index("fsdp")
    spots = [position_of(index % 2, bits, me) for index in range(pairs)]
    locals_ = []
    for index in range(pairs):
        copy = pltpu.make_async_copy(own[index], out[index].at[spots[index]], local_sem.at[index])
        copy.start()
        locals_.append(copy)
    meet(bits, me)
    for copy in locals_:
        copy.wait()
    sends = []

    def send(index, step):
        bit = part_order(index % 2, bits)[bits - 1 - step]
        size = 2**step
        region = out[index].at[pl.ds(spots[index] // size * size, size)]
        copy = pltpu.make_async_remote_copy(
            src_ref=region,
            dst_ref=region,
            send_sem=send_sem.at[index, step],
            recv_sem=recv_sem.at[index, step],
            device_id=(across(me, bit),),
            device_id_type=pl.DeviceIdType.MESH,
        )
        copy.start()
        sends.append(copy)
        return copy

    flying = [send(index, 0) for index in range(pairs)]
    for step in range(bits):
        for index in range(pairs):
            flying[index].wait_recv()
            if step + 1 < bits:
                flying[index] = send(index, step + 1)
    for copy in sends:
        copy.wait_send()


def scatter_kernel(bits, *refs):
    pairs = LAYERS * 2
    packed, out = refs[:pairs], refs[pairs : pairs + LAYERS]
    landed = refs[pairs + LAYERS : pairs + LAYERS + pairs * bits]
    send_sem, recv_sem = refs[pairs + LAYERS + pairs * bits :]
    me = lax.axis_index("fsdp")
    meet(bits, me)
    sends = []

    def source(index, step):
        return packed[index] if step == 0 else landed[index * bits + step - 1]

    def mine(index, step):
        return me // 2 ** part_order(index % 2, bits)[step] % 2

    def send(index, step):
        half = 2 ** (bits - 1 - step)
        copy = pltpu.make_async_remote_copy(
            src_ref=source(index, step).at[pl.ds((1 - mine(index, step)) * half, half)],
            dst_ref=landed[index * bits + step],
            send_sem=send_sem.at[index, step],
            recv_sem=recv_sem.at[index, step],
            device_id=(across(me, part_order(index % 2, bits)[step]),),
            device_id_type=pl.DeviceIdType.MESH,
        )
        copy.start()
        sends.append(copy)
        return copy

    flying = [send(index, 0) for index in range(pairs)]
    for step in range(bits):
        half = 2 ** (bits - 1 - step)
        for index in range(pairs):
            flying[index].wait_recv()
            here, before = landed[index * bits + step], source(index, step)
            base = mine(index, step) * half
            if step + 1 < bits:

                def add(block, carry, here=here, before=before, base=base):
                    here[block] = (here[block].astype(F32) + before[base + block].astype(F32)).astype(
                        BF16
                    )
                    return carry

                lax.fori_loop(0, half, add, 0)
                flying[index] = send(index, step + 1)
            else:
                rows = here.shape[1]
                start = 0 if index % 2 == 0 else out[0].shape[0] - rows
                out[index // 2][start : start + rows, :] = here[0].astype(F32) + before[base].astype(F32)
    for copy in sends:
        copy.wait_send()


def unpack(gathered, owned, flat, mats, vecs):
    devices = gathered[0].shape[0]
    bits = devices.bit_length() - 1
    top = gathered[0].shape[1]

    def widen(position, carry):
        first = owner_of(0, bits, position) * owned
        flat[pl.ds(first, top), :] = gathered[0][position].astype(F32)
        second = owner_of(1, bits, position) * owned + top
        flat[pl.ds(second, owned - top), :] = gathered[1][position].astype(F32)[: owned - top]
        return carry

    lax.fori_loop(0, devices, widen, 0)
    for block in range(BLOCKS):
        for tile in range(SUB):
            start, stride = block_rows(block, tile)
            mats[block, :, tile * LANES : (tile + 1) * LANES] = flat[
                pl.ds(start, D, stride=stride), :
            ].astype(BF16)
    for vector in range(VECTORS):
        for tile in range(SUB):
            row = AT_SMALL + vector * SUB + tile
            vecs[vector : vector + 1, tile * LANES : (tile + 1) * LANES] = flat[row : row + 1, :]


def put_block(flat, block, value):
    for tile in range(SUB):
        start, stride = block_rows(block, tile)
        flat[pl.ds(start, D, stride=stride), :] = value[:, tile * LANES : (tile + 1) * LANES]


def put_vector(flat, vector, value):
    for tile in range(SUB):
        row = AT_SMALL + vector * SUB + tile
        flat[row : row + 1, :] = value[:, tile * LANES : (tile + 1) * LANES]


def col_sum(value):
    return jnp.sum(value, axis=0, keepdims=True)


def normalize(rows_in):
    centre = rows_in - jnp.mean(rows_in, axis=-1, keepdims=True)
    spread = lax.rsqrt(jnp.mean(centre * centre, axis=-1, keepdims=True) + EPS_NORM)
    return centre * spread, spread


def normalize_back(upstream, normed, spread, gain_vec):
    scaled = upstream * gain_vec
    centred = (
        scaled
        - jnp.mean(scaled, axis=-1, keepdims=True)
        - normed * jnp.mean(scaled * normed, axis=-1, keepdims=True)
    )
    return spread * centred


def lane_pick(half):
    lane = lax.broadcasted_iota(jnp.int32, (ROWS, LANES), 1)
    return (lane < HEAD_DIM) if half == 0 else (lane >= HEAD_DIM)


def pick(value, half):
    return jnp.where(lane_pick(half), value, jnp.zeros_like(value))


def forward(slots, stream, mats, vecs, saves):
    query, key, value, attended, exact, middle, slope, hidden = saves

    def vec(index):
        return vecs[index : index + 1, :]

    normed, _ = normalize(stream[...].astype(F32))
    act = (normed * vec(G_ONE) + vec(B_ONE)).astype(BF16)
    query[...] = (nn(act, mats[0]) + vec(B_QUERY)).astype(BF16)
    key[...] = nn(act, mats[1]).astype(BF16)
    value[...] = (nn(act, mats[2]) + vec(B_VALUE)).astype(BF16)

    def heads(pair, carry):
        lanes = pl.ds(pl.multiple_of(pair * LANES, LANES), LANES)
        inside = lax.broadcasted_iota(jnp.int32, (ROWS, ROWS), 1) < SEQ
        for slot in range(slots):
            rows = pl.ds(slot * ROWS, ROWS)
            q_pair, k_pair, v_pair = query[rows, lanes], key[rows, lanes], value[rows, lanes]
            total = jnp.zeros((ROWS, LANES), F32)
            for half in range(2):
                scores = nt(pick(q_pair, half), k_pair) * HEAD_DIM ** (-0.5)
                scores = jnp.where(inside, scores, -1e30)
                expd = jnp.exp(scores - jnp.max(scores, axis=-1, keepdims=True))
                probs = expd * (1.0 / jnp.sum(expd, axis=-1, keepdims=True))
                exact[pair * (2 * slots) + 2 * slot + half] = probs
                total += pick(nn(probs.astype(BF16), v_pair), half)
            attended[rows, lanes] = total.astype(BF16)
        return carry

    lax.fori_loop(0, HEADS // 2, heads, 0)
    middle[...] = stream[...].astype(F32) + nn(attended[...], mats[3]) + vec(B_OUT)
    normed, _ = normalize(middle[...])
    act = (normed * vec(G_TWO) + vec(B_TWO)).astype(BF16)

    result = middle[...] + vec(B_MLP)
    for chunk in range(CHUNKS):
        pre = nn(act, mats[4 + chunk]) + vec(B_HIDDEN + chunk)
        below = 0.5 * (1.0 + lax.erf(pre * INV_ROOT_TWO))
        hidden[chunk] = (pre * below).astype(BF16)
        slope[chunk] = below + pre * INV_ROOT_TAU * jnp.exp(-0.5 * pre * pre)
        result += nn(hidden[chunk], mats[4 + CHUNKS + chunk])
    return result


def backward(slots, upstream, stream, mats, vecs, saves, flat, mixed, att_grad):
    query, key, value, attended, exact, middle, slope, hidden = saves

    def vec(index):
        return vecs[index : index + 1, :]

    grad = upstream[...]
    up_bf = grad.astype(BF16)
    put_vector(flat, B_MLP, col_sum(grad))
    normed, spread = normalize(middle[...])
    act = (normed * vec(G_TWO) + vec(B_TWO)).astype(BF16)
    into = jnp.zeros_like(grad)
    for chunk in range(CHUNKS):
        hidden_grad = nt(up_bf, mats[4 + CHUNKS + chunk]) * slope[chunk]
        hidden_bf = hidden_grad.astype(BF16)
        put_vector(flat, B_HIDDEN + chunk, col_sum(hidden_grad))
        put_block(flat, 4 + CHUNKS + chunk, tn(hidden[chunk], up_bf))
        put_block(flat, 4 + chunk, tn(act, hidden_bf))
        into += nt(hidden_bf, mats[4 + chunk])
    put_vector(flat, G_TWO, col_sum(into * normed))
    put_vector(flat, B_TWO, col_sum(into))
    middle[...] = grad + normalize_back(into, normed, spread, vec(G_TWO))
    middle_bf = middle[...].astype(BF16)
    put_vector(flat, B_OUT, col_sum(middle[...]))
    put_block(flat, 3, tn(attended[...], middle_bf))
    att_grad[...] = nt(middle_bf, mats[3]).astype(BF16)

    def heads(pair, carry):
        lanes = pl.ds(pl.multiple_of(pair * LANES, LANES), LANES)
        q_sum = jnp.zeros((1, LANES), F32)
        v_sum = jnp.zeros((1, LANES), F32)
        for slot in range(slots):
            rows = pl.ds(slot * ROWS, ROWS)
            q_pair, k_pair, v_pair = query[rows, lanes], key[rows, lanes], value[rows, lanes]
            out_pair = att_grad[rows, lanes]
            q_grad = jnp.zeros((ROWS, LANES), F32)
            k_grad = jnp.zeros((ROWS, LANES), F32)
            v_grad = jnp.zeros((ROWS, LANES), F32)
            for half in range(2):
                probs = exact[pair * (2 * slots) + 2 * slot + half]
                out_half = pick(out_pair, half)
                v_grad += tn(probs.astype(BF16), out_half)
                prob_grad = nt(out_half, v_pair)
                inner = jnp.sum(prob_grad * probs, axis=-1, keepdims=True)
                score_grad = (probs * (prob_grad - inner) * HEAD_DIM ** (-0.5)).astype(BF16)
                q_grad += nn(score_grad, pick(k_pair, half))
                k_grad += tn(score_grad, pick(q_pair, half))
            q_sum += col_sum(q_grad)
            v_sum += col_sum(v_grad)
            mixed[0, rows, lanes] = q_grad.astype(BF16)
            mixed[1, rows, lanes] = k_grad.astype(BF16)
            mixed[2, rows, lanes] = v_grad.astype(BF16)
        flat[pl.ds(AT_SMALL + B_QUERY * SUB + pair, 1), :] = q_sum
        flat[pl.ds(AT_SMALL + B_VALUE * SUB + pair, 1), :] = v_sum
        return carry

    lax.fori_loop(0, HEADS // 2, heads, 0)
    normed, spread = normalize(stream[...].astype(F32))
    act = (normed * vec(G_ONE) + vec(B_ONE)).astype(BF16)
    into = jnp.zeros_like(grad)
    for part in range(3):
        put_block(flat, part, tn(act, mixed[part]))
        into += nt(mixed[part], mats[part])
    put_vector(flat, G_ONE, col_sum(into * normed))
    put_vector(flat, B_ONE, col_sum(into))
    return middle[...] + normalize_back(into, normed, spread, vec(G_ONE))


def send_out(flat, packed):
    devices, top = packed[0].shape[0], packed[0].shape[1]
    bits = devices.bit_length() - 1
    owned = flat.shape[0] // devices
    spare = top + packed[1].shape[1] - owned
    flat[USED:, :] = jnp.zeros((flat.shape[0] - USED, LANES), F32)

    def narrow(position, carry):
        first = owner_of(0, bits, position) * owned
        packed[0][position] = flat[pl.ds(first, top), :].astype(BF16)
        second = owner_of(1, bits, position) * owned + top
        packed[1][position, : owned - top, :] = flat[pl.ds(second, owned - top), :].astype(BF16)
        if spare > 0:
            packed[1][position, owned - top :, :] = jnp.zeros((spare, LANES), BF16)
        return carry

    lax.fori_loop(0, devices, narrow, 0)


def save_shapes(slots):
    tokens = slots * ROWS
    return [
        ((tokens, D), BF16),
        ((tokens, D), BF16),
        ((tokens, D), BF16),
        ((tokens, D), BF16),
        ((HEADS * slots, ROWS, ROWS), F32),
        ((tokens, D), F32),
        ((CHUNKS, tokens, D), F32),
        ((CHUNKS, tokens, D), BF16),
    ]


WEIGHTS = [((BLOCKS, D, D), BF16), ((16, D), F32)]


def first_kernel(slots, owned, top, bottom, stream, *rest):
    mats, vecs, *saves = rest[:10]
    result, flat = rest[10:]
    unpack((top, bottom), owned, flat, mats, vecs)
    result[...] = forward(slots, stream, mats, vecs, saves)


def turn_kernel(slots, owned, top, bottom, stream, upstream, result, down, *rest):
    packed, (flat, mixed, att_grad, mats, vecs, *saves) = rest[:2], rest[2:]
    unpack((top, bottom), owned, flat, mats, vecs)
    result[...] = forward(slots, stream, mats, vecs, saves)
    down[...] = backward(
        slots, upstream, stream, mats, vecs, saves, flat, mixed, att_grad
    )
    send_out(flat, packed)


def last_kernel(slots, upstream, stream, *rest):
    mats, vecs, *saved = rest[:10]
    down, top, bottom, flat, mixed, att_grad, middle = rest[10:]
    middle[...] = saved[5][...]
    saved[5] = middle
    down[...] = backward(
        slots, upstream, stream, mats, vecs, saved, flat, mixed, att_grad
    )
    send_out(flat, (top, bottom))


def shapes(listed):
    return [jax.ShapeDtypeStruct(extent, kind) for extent, kind in listed]


def scratch(listed):
    return [pltpu.VMEM(extent, kind) for extent, kind in listed]


def call(body, args, outs, scratches, flops, ident=None):
    whole = pl.BlockSpec(memory_space=pltpu.VMEM)
    extra = {} if ident is None else dict(collective_id=ident, has_side_effects=True)
    return pl.pallas_call(
        body,
        out_shape=shapes(outs),
        in_specs=[whole] * len(args),
        out_specs=[whole] * len(outs),
        scratch_shapes=scratches,
        cost_estimate=pl.CostEstimate(flops=flops, bytes_accessed=12000000, transcendentals=0),
        compiler_params=pltpu.CompilerParams(vmem_limit_bytes=60000000, **extra),
    )(*args)


def adamw(weights_in, first_in, second_in, grad_in):
    first_new = BETA_ONE * first_in + (1.0 - BETA_ONE) * grad_in
    second_new = BETA_TWO * second_in + (1.0 - BETA_TWO) * grad_in * grad_in
    first_hat = first_new / (1.0 - BETA_ONE**ADAM_STEP)
    second_hat = second_new / (1.0 - BETA_TWO**ADAM_STEP)
    updated = weights_in - LEARN * (
        first_hat / (jnp.sqrt(second_hat) + ADAM_EPS) + DECAY * weights_in
    )
    return (updated, first_new, second_new)


def on_device(images, cotangent, counts, params, moment_one, moment_two):
    slots = images.shape[0]
    shard_len = params.shape[1]
    devices = lax.axis_size("fsdp")
    owned = shard_len // LANES
    bits = devices.bit_length() - 1
    padded = -(-owned // 16) * 16
    top = padded // 32 * 16
    tokens = slots * ROWS
    flat_rows = owned * devices
    live = (jnp.arange(slots) < counts[0]).astype(F32)[:, None, None]
    own = jnp.pad(
        params.astype(BF16).reshape(LAYERS, owned, LANES), ((0, 0), (0, padded - owned), (0, 0))
    )
    halves = [((devices, top, LANES), BF16), ((devices, padded - top, LANES), BF16)]
    many = (LAYERS * 2, bits)
    gathered = call(
        functools.partial(gather_kernel, bits),
        [piece for position in range(LAYERS) for piece in (own[position, :top], own[position, top:])],
        halves * LAYERS,
        [
            pltpu.SemaphoreType.DMA((LAYERS * 2,)),
            pltpu.SemaphoreType.DMA(many),
            pltpu.SemaphoreType.DMA(many),
        ],
        0,
        0,
    )
    widen = ((0, 0), (0, ROWS - SEQ), (0, 0))
    start = jnp.pad(images, widen).reshape(tokens, D)
    upstream = jnp.pad(cotangent * live, widen).reshape(tokens, D)

    saves = save_shapes(slots)
    rows_out = ((tokens, D), F32)
    flat = ((flat_rows, LANES), F32)
    back = [flat, ((3, tokens, D), BF16), ((tokens, D), BF16)]
    flops = 2 * tokens * USED * LANES

    *kept, stream = call(
        functools.partial(first_kernel, slots, owned),
        [*gathered[:2], start],
        WEIGHTS + saves + [rows_out],
        scratch([flat]),
        flops,
    )
    result, down, *packed_one = call(
        functools.partial(turn_kernel, slots, owned),
        [*gathered[2:], stream, upstream],
        [rows_out, rows_out] + halves,
        scratch(back + WEIGHTS + saves),
        3 * flops,
    )
    down, *packed_zero = call(
        functools.partial(last_kernel, slots),
        [down, start] + kept,
        [rows_out] + halves,
        scratch(back + [rows_out]),
        2 * flops,
    )
    landing = [
        ((2 ** (bits - 1 - step), rows, LANES), BF16)
        for _ in range(LAYERS)
        for rows in (top, padded - top)
        for step in range(bits)
    ]
    sums = call(
        functools.partial(scatter_kernel, bits),
        [*packed_zero, *packed_one],
        [((padded, LANES), F32)] * LAYERS,
        scratch(landing) + [pltpu.SemaphoreType.DMA(many), pltpu.SemaphoreType.DMA(many)],
        0,
        1,
    )
    grad_stack = jnp.stack([total[:owned].reshape(-1) for total in sums])
    updated, first_new, second_new = adamw(params, moment_one, moment_two, grad_stack)
    return (
        result.reshape(slots, ROWS, D)[:, :SEQ] * live,
        down.reshape(slots, ROWS, D)[:, :SEQ],
        grad_stack,
        updated,
        first_new,
        second_new,
    )


def solution(mesh):
    placed = (
        P("fsdp", None, None),
        P("fsdp", None, None),
        P("fsdp"),
        P(None, "fsdp"),
        P(None, "fsdp"),
        P(None, "fsdp"),
    )
    return jax.shard_map(
        on_device,
        mesh=mesh,
        in_specs=placed,
        out_specs=(
            P("fsdp", None, None),
            P("fsdp", None, None),
            P(None, "fsdp"),
            P(None, "fsdp"),
            P(None, "fsdp"),
            P(None, "fsdp"),
        ),
        check_vma=False,
    )
```

```python
import functools
import math

import jax
import jax.numpy as jnp
from jax import lax
from jax.experimental import pallas as pl
from jax.experimental.pallas import tpu as pltpu
from jax.sharding import PartitionSpec as P

D = 384
HEADS = 6
HEAD_DIM = 64
FF = 1536
SEQ = 197
LAYERS = 2
ADAM_STEP = 4

EPS_NORM = 1e-06
BETA_ONE = 0.9
BETA_TWO = 0.999
ADAM_EPS = 1e-08
DECAY = 0.05
LEARN = 0.2
INV_ROOT_TWO = 0.7071067811865476
INV_ROOT_TAU = 0.3989422804014327
LANES = 128
ROWS = 208
SUB = D // LANES
CHUNKS = FF // D
F32 = jnp.float32
BF16 = jnp.bfloat16

AT_OUT = 3 * D * SUB
AT_ONE = AT_OUT + D * SUB
AT_TWO = AT_ONE + D * SUB * CHUNKS
AT_SMALL = AT_TWO + D * SUB * CHUNKS
BLOCKS = 4 + 2 * CHUNKS
G_ONE, B_ONE, B_QUERY, B_VALUE, B_OUT, G_TWO, B_TWO, B_HIDDEN = range(8)
B_MLP = B_HIDDEN + CHUNKS
VECTORS = B_MLP + 1
USED = AT_SMALL + VECTORS * SUB


def nn(left, right):
    return jnp.dot(left, right, preferred_element_type=F32)


def nt(left, right):
    return lax.dot_general(left, right, (((1,), (1,)), ((), ())), preferred_element_type=F32)


def tn(left, right):
    return lax.dot_general(left, right, (((0,), (0,)), ((), ())), preferred_element_type=F32)


def block_rows(block, tile):
    if block < 3:
        return block * SUB + tile, 3 * SUB
    if block == 3:
        return AT_OUT + tile, SUB
    if block < 4 + CHUNKS:
        return AT_ONE + (block - 4) * SUB + tile, CHUNKS * SUB
    return AT_TWO + (block - 4 - CHUNKS) * D * SUB + tile, SUB


def part_order(part, bits):
    order = list(range(bits))
    if part == 1 and bits > 2:
        order[1], order[2] = 2, 1
    return order


def owner_of(part, bits, position):
    owner = 0
    for place, bit in enumerate(part_order(part, bits)):
        owner = owner + (position // 2 ** (bits - 1 - place)) % 2 * 2**bit
    return owner


def position_of(part, bits, device):
    position = 0
    for place, bit in enumerate(part_order(part, bits)):
        position = position + device // 2**bit % 2 * 2 ** (bits - 1 - place)
    return position


def meet(bits, me):
    barrier = pltpu.get_barrier_semaphore()
    for bit in range(bits):
        pl.semaphore_signal(
            barrier, inc=1, device_id=(across(me, bit),), device_id_type=pl.DeviceIdType.MESH
        )
    pl.semaphore_wait(barrier, bits)


def across(me, bit):
    return me + 2**bit * (1 - 2 * (me // 2**bit % 2))


def gather_steps(bits, own, out, local_sem, send_sem, recv_sem):
    pairs = LAYERS * 2
    me = lax.axis_index("fsdp")
    spots = [position_of(index % 2, bits, me) for index in range(pairs)]
    locals_ = []
    for index in range(pairs):
        copy = pltpu.make_async_copy(own[index], out[index].at[spots[index]], local_sem.at[index])
        copy.start()
        locals_.append(copy)
    meet(bits, me)
    for copy in locals_:
        copy.wait()
    sends = []

    def send(index, step):
        bit = part_order(index % 2, bits)[bits - 1 - step]
        size = 2**step
        region = out[index].at[pl.ds(spots[index] // size * size, size)]
        copy = pltpu.make_async_remote_copy(
            src_ref=region,
            dst_ref=region,
            send_sem=send_sem.at[index, step],
            recv_sem=recv_sem.at[index, step],
            device_id=(across(me, bit),),
            device_id_type=pl.DeviceIdType.MESH,
        )
        copy.start()
        sends.append(copy)
        return copy

    flying = [send(index, 0) for index in range(pairs)]
    schedule = [(index, step) for step in range(bits - 2) for index in range(pairs)]
    schedule += [(index, step) for step in (bits - 2, bits - 1) for index in range(2)]
    for index, step in schedule:
        flying[index].wait_recv()
        if step + 1 < bits:
            flying[index] = send(index, step + 1)
    yield
    for step in (bits - 2, bits - 1):
        for index in range(2, pairs):
            flying[index].wait_recv()
            if step + 1 < bits:
                flying[index] = send(index, step + 1)
        if step == bits - 2:
            yield
    for copy in sends:
        copy.wait_send()
    yield


def scatter_kernel(bits, *refs):
    pairs = LAYERS * 2
    packed, out = refs[:pairs], refs[pairs : pairs + LAYERS]
    landed = refs[pairs + LAYERS : pairs + LAYERS + pairs * bits]
    send_sem, recv_sem = refs[pairs + LAYERS + pairs * bits :]
    me = lax.axis_index("fsdp")
    meet(bits, me)
    sends = []

    def source(index, step):
        return packed[index] if step == 0 else landed[index * bits + step - 1]

    def mine(index, step):
        return me // 2 ** part_order(index % 2, bits)[step] % 2

    def send(index, step):
        half = 2 ** (bits - 1 - step)
        copy = pltpu.make_async_remote_copy(
            src_ref=source(index, step).at[pl.ds((1 - mine(index, step)) * half, half)],
            dst_ref=landed[index * bits + step],
            send_sem=send_sem.at[index, step],
            recv_sem=recv_sem.at[index, step],
            device_id=(across(me, part_order(index % 2, bits)[step]),),
            device_id_type=pl.DeviceIdType.MESH,
        )
        copy.start()
        sends.append(copy)
        return copy

    flying = [send(index, 0) for index in range(pairs)]
    for step in range(bits):
        half = 2 ** (bits - 1 - step)
        for index in range(pairs):
            flying[index].wait_recv()
            here, before = landed[index * bits + step], source(index, step)
            base = mine(index, step) * half
            if step + 1 < bits:

                def add(block, carry, here=here, before=before, base=base):
                    here[block] = (here[block].astype(F32) + before[base + block].astype(F32)).astype(
                        BF16
                    )
                    return carry

                lax.fori_loop(0, half, add, 0)
                flying[index] = send(index, step + 1)
            else:
                rows = here.shape[1]
                start = 0 if index % 2 == 0 else out[0].shape[0] - rows
                out[index // 2][start : start + rows, :] = here[0].astype(F32) + before[base].astype(F32)
    for copy in sends:
        copy.wait_send()


def unpack(gathered, owned, flat, mats, vecs):
    devices = gathered[0].shape[0]
    bits = devices.bit_length() - 1
    top = gathered[0].shape[1]

    def widen(position, carry):
        first = owner_of(0, bits, position) * owned
        flat[pl.ds(first, top), :] = gathered[0][position].astype(F32)
        second = owner_of(1, bits, position) * owned + top
        flat[pl.ds(second, owned - top), :] = gathered[1][position].astype(F32)[: owned - top]
        return carry

    lax.fori_loop(0, devices, widen, 0)
    for block in range(BLOCKS):
        for tile in range(SUB):
            start, stride = block_rows(block, tile)
            mats[block, :, tile * LANES : (tile + 1) * LANES] = flat[
                pl.ds(start, D, stride=stride), :
            ].astype(BF16)
    for vector in range(VECTORS):
        for tile in range(SUB):
            row = AT_SMALL + vector * SUB + tile
            vecs[vector : vector + 1, tile * LANES : (tile + 1) * LANES] = flat[row : row + 1, :]


def put_block(flat, block, value):
    for tile in range(SUB):
        start, stride = block_rows(block, tile)
        flat[pl.ds(start, D, stride=stride), :] = value[:, tile * LANES : (tile + 1) * LANES]


def put_vector(flat, vector, value):
    for tile in range(SUB):
        row = AT_SMALL + vector * SUB + tile
        flat[row : row + 1, :] = value[:, tile * LANES : (tile + 1) * LANES]


def col_sum(value):
    return jnp.sum(value, axis=0, keepdims=True)


def normalize(rows_in):
    centre = rows_in - jnp.mean(rows_in, axis=-1, keepdims=True)
    spread = lax.rsqrt(jnp.mean(centre * centre, axis=-1, keepdims=True) + EPS_NORM)
    return centre * spread, spread


def normalize_back(upstream, normed, spread, gain_vec):
    scaled = upstream * gain_vec
    centred = (
        scaled
        - jnp.mean(scaled, axis=-1, keepdims=True)
        - normed * jnp.mean(scaled * normed, axis=-1, keepdims=True)
    )
    return spread * centred


def lane_pick(half):
    lane = lax.broadcasted_iota(jnp.int32, (ROWS, LANES), 1)
    return (lane < HEAD_DIM) if half == 0 else (lane >= HEAD_DIM)


def pick(value, half):
    return jnp.where(lane_pick(half), value, jnp.zeros_like(value))


def forward(slots, stream, mats, vecs, saves, tick=None):
    query, key, value, attended, exact, middle, slope, hidden = saves

    def vec(index):
        return vecs[index : index + 1, :]

    normed, _ = normalize(stream[...].astype(F32))
    act = (normed * vec(G_ONE) + vec(B_ONE)).astype(BF16)
    query[...] = (nn(act, mats[0]) + vec(B_QUERY)).astype(BF16)
    key[...] = nn(act, mats[1]).astype(BF16)
    value[...] = (nn(act, mats[2]) + vec(B_VALUE)).astype(BF16)

    def heads(pair, carry):
        lanes = pl.ds(pl.multiple_of(pair * LANES, LANES), LANES)
        inside = lax.broadcasted_iota(jnp.int32, (ROWS, ROWS), 1) < SEQ
        for slot in range(slots):
            rows = pl.ds(slot * ROWS, ROWS)
            q_pair, k_pair, v_pair = query[rows, lanes], key[rows, lanes], value[rows, lanes]
            total = jnp.zeros((ROWS, LANES), F32)
            for half in range(2):
                scores = nt(pick(q_pair, half), k_pair) * HEAD_DIM ** (-0.5)
                scores = jnp.where(inside, scores, -1e30)
                expd = jnp.exp(scores - jnp.max(scores, axis=-1, keepdims=True))
                probs = expd * (1.0 / jnp.sum(expd, axis=-1, keepdims=True))
                exact[pair * (2 * slots) + 2 * slot + half] = probs
                total += pick(nn(probs.astype(BF16), v_pair), half)
            attended[rows, lanes] = total.astype(BF16)
        return carry

    lax.fori_loop(0, HEADS // 2, heads, 0)
    if tick is not None:
        tick()
    middle[...] = stream[...].astype(F32) + nn(attended[...], mats[3]) + vec(B_OUT)
    normed, _ = normalize(middle[...])
    act = (normed * vec(G_TWO) + vec(B_TWO)).astype(BF16)

    result = middle[...] + vec(B_MLP)
    for chunk in range(CHUNKS):
        pre = nn(act, mats[4 + chunk]) + vec(B_HIDDEN + chunk)
        below = 0.5 * (1.0 + lax.erf(pre * INV_ROOT_TWO))
        hidden[chunk] = (pre * below).astype(BF16)
        slope[chunk] = below + pre * INV_ROOT_TAU * jnp.exp(-0.5 * pre * pre)
        result += nn(hidden[chunk], mats[4 + CHUNKS + chunk])
    return result


def backward(slots, upstream, stream, mats, vecs, saves, flat, mixed, att_grad):
    query, key, value, attended, exact, middle, slope, hidden = saves

    def vec(index):
        return vecs[index : index + 1, :]

    grad = upstream[...]
    up_bf = grad.astype(BF16)
    put_vector(flat, B_MLP, col_sum(grad))
    normed, spread = normalize(middle[...])
    act = (normed * vec(G_TWO) + vec(B_TWO)).astype(BF16)
    into = jnp.zeros_like(grad)
    for chunk in range(CHUNKS):
        hidden_grad = nt(up_bf, mats[4 + CHUNKS + chunk]) * slope[chunk]
        hidden_bf = hidden_grad.astype(BF16)
        put_vector(flat, B_HIDDEN + chunk, col_sum(hidden_grad))
        put_block(flat, 4 + CHUNKS + chunk, tn(hidden[chunk], up_bf))
        put_block(flat, 4 + chunk, tn(act, hidden_bf))
        into += nt(hidden_bf, mats[4 + chunk])
    put_vector(flat, G_TWO, col_sum(into * normed))
    put_vector(flat, B_TWO, col_sum(into))
    middle[...] = grad + normalize_back(into, normed, spread, vec(G_TWO))
    middle_bf = middle[...].astype(BF16)
    put_vector(flat, B_OUT, col_sum(middle[...]))
    put_block(flat, 3, tn(attended[...], middle_bf))
    att_grad[...] = nt(middle_bf, mats[3]).astype(BF16)

    def heads(pair, carry):
        lanes = pl.ds(pl.multiple_of(pair * LANES, LANES), LANES)
        q_sum = jnp.zeros((1, LANES), F32)
        v_sum = jnp.zeros((1, LANES), F32)
        for slot in range(slots):
            rows = pl.ds(slot * ROWS, ROWS)
            q_pair, k_pair, v_pair = query[rows, lanes], key[rows, lanes], value[rows, lanes]
            out_pair = att_grad[rows, lanes]
            q_grad = jnp.zeros((ROWS, LANES), F32)
            k_grad = jnp.zeros((ROWS, LANES), F32)
            v_grad = jnp.zeros((ROWS, LANES), F32)
            for half in range(2):
                probs = exact[pair * (2 * slots) + 2 * slot + half]
                out_half = pick(out_pair, half)
                v_grad += tn(probs.astype(BF16), out_half)
                prob_grad = nt(out_half, v_pair)
                inner = jnp.sum(prob_grad * probs, axis=-1, keepdims=True)
                score_grad = (probs * (prob_grad - inner) * HEAD_DIM ** (-0.5)).astype(BF16)
                q_grad += nn(score_grad, pick(k_pair, half))
                k_grad += tn(score_grad, pick(q_pair, half))
            q_sum += col_sum(q_grad)
            v_sum += col_sum(v_grad)
            mixed[0, rows, lanes] = q_grad.astype(BF16)
            mixed[1, rows, lanes] = k_grad.astype(BF16)
            mixed[2, rows, lanes] = v_grad.astype(BF16)
        flat[pl.ds(AT_SMALL + B_QUERY * SUB + pair, 1), :] = q_sum
        flat[pl.ds(AT_SMALL + B_VALUE * SUB + pair, 1), :] = v_sum
        return carry

    lax.fori_loop(0, HEADS // 2, heads, 0)
    normed, spread = normalize(stream[...].astype(F32))
    act = (normed * vec(G_ONE) + vec(B_ONE)).astype(BF16)
    into = jnp.zeros_like(grad)
    for part in range(3):
        put_block(flat, part, tn(act, mixed[part]))
        into += nt(mixed[part], mats[part])
    put_vector(flat, G_ONE, col_sum(into * normed))
    put_vector(flat, B_ONE, col_sum(into))
    return middle[...] + normalize_back(into, normed, spread, vec(G_ONE))


def send_out(flat, packed):
    devices, top = packed[0].shape[0], packed[0].shape[1]
    bits = devices.bit_length() - 1
    owned = flat.shape[0] // devices
    spare = top + packed[1].shape[1] - owned
    flat[USED:, :] = jnp.zeros((flat.shape[0] - USED, LANES), F32)

    def narrow(position, carry):
        first = owner_of(0, bits, position) * owned
        packed[0][position] = flat[pl.ds(first, top), :].astype(BF16)
        second = owner_of(1, bits, position) * owned + top
        packed[1][position, : owned - top, :] = flat[pl.ds(second, owned - top), :].astype(BF16)
        if spare > 0:
            packed[1][position, owned - top :, :] = jnp.zeros((spare, LANES), BF16)
        return carry

    lax.fori_loop(0, devices, narrow, 0)


def save_shapes(slots):
    tokens = slots * ROWS
    return [
        ((tokens, D), BF16),
        ((tokens, D), BF16),
        ((tokens, D), BF16),
        ((tokens, D), BF16),
        ((HEADS * slots, ROWS, ROWS), F32),
        ((tokens, D), F32),
        ((CHUNKS, tokens, D), F32),
        ((CHUNKS, tokens, D), BF16),
    ]


WEIGHTS = [((BLOCKS, D, D), BF16), ((16, D), F32)]


def first_kernel(slots, owned, bits, *refs):
    own, stream, after = refs[:4], refs[4], refs[5:7]
    mats, vecs, *saves = refs[7:17]
    result, flat = refs[17:19]
    before = refs[19:21]
    steps = gather_steps(bits, own, [*before, *after], *refs[21:])
    next(steps)
    unpack(before, owned, flat, mats, vecs)
    result[...] = forward(slots, stream, mats, vecs, saves, lambda: next(steps))
    next(steps)


def turn_kernel(slots, owned, top, bottom, stream, upstream, result, down, *rest):
    packed, (flat, mixed, att_grad, mats, vecs, *saves) = rest[:2], rest[2:]
    unpack((top, bottom), owned, flat, mats, vecs)
    result[...] = forward(slots, stream, mats, vecs, saves)
    down[...] = backward(
        slots, upstream, stream, mats, vecs, saves, flat, mixed, att_grad
    )
    send_out(flat, packed)


def last_kernel(slots, upstream, stream, *rest):
    mats, vecs, *saved = rest[:10]
    down, top, bottom, flat, mixed, att_grad, middle = rest[10:]
    middle[...] = saved[5][...]
    saved[5] = middle
    down[...] = backward(
        slots, upstream, stream, mats, vecs, saved, flat, mixed, att_grad
    )
    send_out(flat, (top, bottom))


def shapes(listed):
    return [jax.ShapeDtypeStruct(extent, kind) for extent, kind in listed]


def scratch(listed):
    return [pltpu.VMEM(extent, kind) for extent, kind in listed]


def call(body, args, outs, scratches, flops, ident=None):
    whole = pl.BlockSpec(memory_space=pltpu.VMEM)
    extra = {} if ident is None else dict(collective_id=ident, has_side_effects=True)
    return pl.pallas_call(
        body,
        out_shape=shapes(outs),
        in_specs=[whole] * len(args),
        out_specs=[whole] * len(outs),
        scratch_shapes=scratches,
        cost_estimate=pl.CostEstimate(flops=flops, bytes_accessed=12000000, transcendentals=0),
        compiler_params=pltpu.CompilerParams(vmem_limit_bytes=60000000, **extra),
    )(*args)


def adamw(weights_in, first_in, second_in, grad_in):
    first_new = BETA_ONE * first_in + (1.0 - BETA_ONE) * grad_in
    second_new = BETA_TWO * second_in + (1.0 - BETA_TWO) * grad_in * grad_in
    first_hat = first_new / (1.0 - BETA_ONE**ADAM_STEP)
    second_hat = second_new / (1.0 - BETA_TWO**ADAM_STEP)
    updated = weights_in - LEARN * (
        first_hat / (jnp.sqrt(second_hat) + ADAM_EPS) + DECAY * weights_in
    )
    return (updated, first_new, second_new)


def on_device(images, cotangent, counts, params, moment_one, moment_two):
    slots = images.shape[0]
    shard_len = params.shape[1]
    devices = lax.axis_size("fsdp")
    owned = shard_len // LANES
    bits = devices.bit_length() - 1
    padded = -(-owned // 16) * 16
    top = padded // 32 * 16
    tokens = slots * ROWS
    flat_rows = owned * devices
    live = (jnp.arange(slots) < counts[0]).astype(F32)[:, None, None]
    own = jnp.pad(
        params.astype(BF16).reshape(LAYERS, owned, LANES), ((0, 0), (0, padded - owned), (0, 0))
    )
    halves = [((devices, top, LANES), BF16), ((devices, padded - top, LANES), BF16)]
    many = (LAYERS * 2, bits)
    widen = ((0, 0), (0, ROWS - SEQ), (0, 0))
    start = jnp.pad(images, widen).reshape(tokens, D)
    upstream = jnp.pad(cotangent * live, widen).reshape(tokens, D)

    saves = save_shapes(slots)
    rows_out = ((tokens, D), F32)
    flat = ((flat_rows, LANES), F32)
    back = [flat, ((3, tokens, D), BF16), ((tokens, D), BF16)]
    flops = 2 * tokens * USED * LANES

    after_top, after_bottom, *kept, stream = call(
        functools.partial(first_kernel, slots, owned, bits),
        [piece for position in range(LAYERS) for piece in (own[position, :top], own[position, top:])]
        + [start],
        halves + WEIGHTS + saves + [rows_out],
        scratch([flat] + halves)
        + [
            pltpu.SemaphoreType.DMA((LAYERS * 2,)),
            pltpu.SemaphoreType.DMA(many),
            pltpu.SemaphoreType.DMA(many),
        ],
        flops,
        0,
    )
    result, down, *packed_one = call(
        functools.partial(turn_kernel, slots, owned),
        [after_top, after_bottom, stream, upstream],
        [rows_out, rows_out] + halves,
        scratch(back + WEIGHTS + saves),
        3 * flops,
    )
    down, *packed_zero = call(
        functools.partial(last_kernel, slots),
        [down, start] + kept,
        [rows_out] + halves,
        scratch(back + [rows_out]),
        2 * flops,
    )
    landing = [
        ((2 ** (bits - 1 - step), rows, LANES), BF16)
        for _ in range(LAYERS)
        for rows in (top, padded - top)
        for step in range(bits)
    ]
    sums = call(
        functools.partial(scatter_kernel, bits),
        [*packed_zero, *packed_one],
        [((padded, LANES), F32)] * LAYERS,
        scratch(landing) + [pltpu.SemaphoreType.DMA(many), pltpu.SemaphoreType.DMA(many)],
        0,
        1,
    )
    grad_stack = jnp.stack([total[:owned].reshape(-1) for total in sums])
    updated, first_new, second_new = adamw(params, moment_one, moment_two, grad_stack)
    return (
        result.reshape(slots, ROWS, D)[:, :SEQ] * live,
        down.reshape(slots, ROWS, D)[:, :SEQ],
        grad_stack,
        updated,
        first_new,
        second_new,
    )


def solution(mesh):
    placed = (
        P("fsdp", None, None),
        P("fsdp", None, None),
        P("fsdp"),
        P(None, "fsdp"),
        P(None, "fsdp"),
        P(None, "fsdp"),
    )
    return jax.shard_map(
        on_device,
        mesh=mesh,
        in_specs=placed,
        out_specs=(
            P("fsdp", None, None),
            P("fsdp", None, None),
            P(None, "fsdp"),
            P(None, "fsdp"),
            P(None, "fsdp"),
            P(None, "fsdp"),
        ),
        check_vma=False,
    )
```
